32 devices in a mesh: groups: 1, fac: 32 (over z, y, x, core).
Axes of the slice: x: 2, y: 2, z: 4, core: 2. Of those that a mesh axis runs over, the one named last changes fastest.
Arguments:
- sky_image: float32 [64, 96, 4096], P(('groups', 'fac')), may hold values from 0 to 18, as said below
- measured_real: float32 [64, 96, 4096], P(('groups', 'fac')), may hold values from -6 to 6
- measured_imaginary: float32 [64, 96, 4096], P(('groups', 'fac')), may hold values from -6 to 6
- sampling_mask: int32 [64, 96, 4096], P(('groups', 'fac')), may hold values 0 or 1
- dual_field: float32 [64, 96, 4096], P('groups', None, 'fac'), may hold values from -6 to 6
Outputs:
- next_image: float32 [64, 96, 4096], P(('groups', 'fac'))
- next_dual: float32 [64, 96, 4096], P('groups', None, 'fac')
The draws below stay inside these ranges and needn't reach their ends.
Inputs may be any that keep to these rules, and one draw needn't show every extreme that they name: `sky_image`: non-negative sky brightness.
All inputs are finite; a program needn't handle non-finite values. No bound on the sum of `sampling_mask` on one device may be relied on, other than what follows from the above.
Results may differ from the reference program's by a relative error of at most 0.00012.
Values sent between devices are 32-bit elements; how exact they have to be, the bound alone decides.
No kernel may reach another device: no remote copies, remote signals or barrier semaphores. Data moves between devices by JAX's collectives and lax.ppermute only.
A program may use at most 192 MiB of HBM per device.

```python
import jax
import jax.numpy as jnp
from jax import lax

CHANNELS = 64
COLUMNS = 4096
ROWS = 96
LEVELS = 4
N_FAC = 32


def draw_sky_image(key, part):
    first_key, second_key = jax.random.split(key, 2)
    channel_scale = jnp.exp(jax.random.uniform(first_key, (CHANNELS, 1, 1), jnp.float32, jnp.log(0.3), jnp.log(3.0)))
    pixels = jnp.exp(jax.random.uniform(second_key, (CHANNELS, ROWS, COLUMNS), jnp.float32, jnp.log(0.1), jnp.log(3.0)))
    return channel_scale * pixels


def set_ends(result, rng, low, largest):
    shape = result.shape
    place = [jax.random.randint(jax.random.fold_in(rng, axis), (), 0, shape[axis]) for axis in range(len(shape))]
    result = result.at[tuple(place)].set(low)
    longest = shape.index(max(shape))
    place[longest] = (place[longest] + 1) % shape[longest]
    return result.at[tuple(place)].set(largest)


def block_levels(stream_key, shape, cuts, smallest, largest):
    def one(position, blocks):
        draws = jax.random.uniform(jax.random.fold_in(jax.random.fold_in(stream_key, 6), position), (blocks,), jnp.float32, smallest / len(cuts), largest / len(cuts))
        return jnp.repeat(jnp.exp(draws), shape[position] // blocks).reshape((-1,) + (1,) * (len(shape) - position - 1))

    gain = one(*cuts[0])
    for cut in cuts[1:]:
        gain = gain * one(*cut)
    return gain


def centred(own_key, extent, scale, limit, cuts=(), kind=jnp.bfloat16):
    level = block_levels(own_key, extent, cuts, -0.22, 0.18) if cuts else 1.0
    result = jax.random.normal(own_key, extent, jnp.float32) * scale * level
    return jnp.minimum(jnp.maximum(result, -limit), limit).astype(kind)


def setup_inputs(seed: int = 0, part: int = 0) -> dict:
    splits = jax.random.split(jax.random.key(seed), 6)
    part_keys = jax.random.split(jax.random.fold_in(splits[5], part), 6)
    sky_image = draw_sky_image(jax.random.fold_in(jax.random.fold_in(splits[5], part), 71), part)
    measured_real = centred(part_keys[1], (CHANNELS, ROWS, COLUMNS), 1.0, 6.0, ((0, 32),), jnp.float32)
    measured_imaginary = centred(part_keys[2], (CHANNELS, ROWS, COLUMNS), 1.0, 6.0, ((0, 32),), jnp.float32)
    sampling_mask = set_ends((jax.random.randint(part_keys[3], (CHANNELS, ROWS, COLUMNS), 0, 2) < 1).astype(jnp.int32), jax.random.fold_in(part_keys[3], 1), 0, 1)
    dual_field = centred(part_keys[4], (CHANNELS, ROWS, COLUMNS), 1.0, 6.0, ((2, 32),), jnp.float32)
    return {"sky_image": sky_image, "measured_real": measured_real, "measured_imaginary": measured_imaginary, "sampling_mask": sampling_mask, "dual_field": dual_field}


low_pass = (0.2303778133088964, 0.7148465705529155, 0.6308807679298587, -0.0279837694168599, -0.1870348117190931, 0.0308413818355607, 0.0328830116668852, -0.010597401785069)
high_pass = tuple(((-1) ** tap_index * low_pass[7 - tap_index] for tap_index in range(8)))
primal_step = 0.6
dual_step = 0.8
ball_radius = 12.0

def split_levels(values):
    coarse = values
    details = []
    for level_index in range(LEVELS):
        length = coarse.shape[-1]
        even_index = 2 * jnp.arange(length // 2, dtype=jnp.int32)
        lower = jnp.zeros(coarse.shape[:-1] + (length // 2,), jnp.float32)
        upper = jnp.zeros(coarse.shape[:-1] + (length // 2,), jnp.float32)
        for tap_index in range(8):
            taken = jnp.take(coarse, (even_index + tap_index) % length, axis=-1)
            lower = lower + low_pass[tap_index] * taken
            upper = upper + high_pass[tap_index] * taken
        details.insert(0, upper)
        coarse = lower
    return [coarse] + details

def wavelet_analysis(values):
    turned = jnp.swapaxes(values, 1, 2)
    row_coeffs = jnp.swapaxes(jnp.concatenate(split_levels(turned), -1), 1, 2)
    pieces = split_levels(row_coeffs)
    facet_major = [piece_part.reshape(piece_part.shape[:-1] + (N_FAC, piece_part.shape[-1] // N_FAC)) for piece_part in pieces]
    return jnp.concatenate(facet_major, -1).reshape(values.shape)

def reference(sky_image, measured_real, measured_imaginary, sampling_mask, dual_field):
    spectrum = jnp.fft.fft2(sky_image, axes=(1, 2), norm='ortho')
    weights = sampling_mask.astype(jnp.float32)
    misfit = weights * (spectrum - (measured_real + 1j * measured_imaginary))
    gradient = jnp.real(jnp.fft.ifft2(misfit, axes=(1, 2), norm='ortho'))
    unused_out, pullback = jax.vjp(wavelet_analysis, jnp.zeros_like(dual_field))
    prior_term = pullback(dual_field)[0]
    next_image = jnp.maximum(sky_image - primal_step * (gradient + prior_term), 0.0)
    lifted = dual_field + dual_step * wavelet_analysis(2.0 * next_image - sky_image)
    channel_norm = jnp.sqrt(lax.optimization_barrier(jnp.sum(lifted * lifted, axis=0)))
    next_dual = lifted / jnp.maximum(1.0, channel_norm / ball_radius)
    return (next_image, next_dual)
```

```python
import functools

import jax
import jax.numpy as jnp
import numpy as np
from jax import lax
from jax.experimental import pallas as pl
from jax.experimental.pallas import tpu as pltpu
from jax.sharding import PartitionSpec as P

LEVELS = 4
LANES = 128

low_pass = (
    0.2303778133088964,
    0.7148465705529155,
    0.6308807679298587,
    -0.0279837694168599,
    -0.1870348117190931,
    0.0308413818355607,
    0.0328830116668852,
    -0.010597401785069,
)
high_pass = tuple(((-1) ** tap_index * low_pass[7 - tap_index] for tap_index in range(8)))
primal_step = 0.6
dual_step = 0.8
ball_radius = 12.0
f32 = jnp.float32
bf16 = jnp.bfloat16


def halves(matrix):
    high = np.asarray(matrix, np.float32).astype(bf16)
    low = (np.asarray(matrix, np.float64) - high.astype(np.float64)).astype(bf16)
    return high, low


def split(values):
    high = values.astype(bf16)
    low = (values - high.astype(f32)).astype(bf16)
    return high, low


def mul(left, right):
    return jnp.dot(left, right, preferred_element_type=f32)


def row_fourier(rows):
    grid = np.arange(rows)
    angles = 2.0 * np.pi * (np.outer(grid, grid) % rows) / rows
    return np.concatenate([np.cos(angles), -np.sin(angles)], 0) / np.sqrt(rows)


def lane_fourier(scale):
    grid = np.arange(LANES)
    angles = 2.0 * np.pi * (np.outer(grid, grid) % LANES) / LANES
    cosine, sine = np.cos(angles), np.sin(angles)
    return np.block([[cosine, -sine], [sine, cosine]]) * scale


def twiddles(slabs, columns):
    angles = 2.0 * np.pi * np.outer(np.arange(slabs), np.arange(LANES)) / columns
    table = np.stack([np.cos(angles), -np.sin(angles)], 1)
    return np.broadcast_to(table[:, :, None, :], (slabs, 2, 8, LANES)).astype(np.float32)


def row_wavelet(length):
    current = np.eye(length)
    details = []
    for level_index in range(LEVELS):
        width_now = current.shape[0]
        half_size = width_now // 2
        lower = np.zeros((half_size, width_now))
        upper = np.zeros((half_size, width_now))
        for target in range(half_size):
            for tap_index in range(8):
                lower[target, (2 * target + tap_index) % width_now] += low_pass[tap_index]
                upper[target, (2 * target + tap_index) % width_now] += high_pass[tap_index]
        details.insert(0, upper @ current)
        current = lower @ current
    return np.concatenate([current] + details, 0)


def facet_wavelet(width):
    needed = [width >> LEVELS]
    for level_index in range(LEVELS):
        needed.insert(0, 2 * (needed[0] - 1) + 8)
    current = np.eye(2 * width)
    details = []
    for level_index in range(LEVELS):
        count = needed[level_index + 1]
        lower = np.zeros((count, 2 * width))
        upper = np.zeros((count, 2 * width))
        for target in range(count):
            for tap_index in range(8):
                lower[target] += low_pass[tap_index] * current[2 * target + tap_index]
                upper[target] += high_pass[tap_index] * current[2 * target + tap_index]
        details.insert(0, upper[: width >> (level_index + 1)])
        current = lower
    matrix = np.concatenate([current[: width >> LEVELS]] + details, 0).T
    return np.concatenate([matrix[:width], matrix[width:]], 1)


def turn(value, step, length, sign):
    real, imag = value
    step = step % length
    if step == 0:
        return real, imag
    if 4 * step == length:
        return (-imag, real) if sign > 0 else (imag, -real)
    if 8 * step == length:
        root = float(np.sqrt(0.5))
        if sign > 0:
            return (real - imag) * root, (real + imag) * root
        return (real + imag) * root, (imag - real) * root
    if 8 * step == 3 * length:
        root = float(np.sqrt(0.5))
        if sign > 0:
            return (real + imag) * (-root), (real - imag) * root
        return (imag - real) * root, (real + imag) * (-root)
    cosine = float(np.cos(2.0 * np.pi * step / length))
    sine = float(sign * np.sin(2.0 * np.pi * step / length))
    return real * cosine - imag * sine, real * sine + imag * cosine


def short_transform(values, sign):
    length = len(values)
    if length == 1:
        return values
    even = short_transform(values[0::2], sign)
    odd = short_transform(values[1::2], sign)
    first, second = [], []
    for step in range(length // 2):
        real, imag = turn(odd[step], step, length, sign)
        first.append((even[step][0] + real, even[step][1] + imag))
        second.append((even[step][0] - real, even[step][1] - imag))
    return first + second


def fidelity_kernel(
    sky, real, imag, mask, row_hi, row_lo, back_hi, back_lo, lane_hi, lane_lo,
    inv_hi, inv_lo, twist, base, row_part, slab_part,
):
    rows, columns = sky.shape[1], sky.shape[2]
    slabs = columns // LANES
    width = 512

    def rows_forward(index, carry):
        lanes = pl.ds(pl.multiple_of(index * width, width), width)
        high, low = split(sky[0, :, lanes])
        row_part[:, lanes] = mul(row_hi[...], high) + mul(row_hi[...], low) + mul(row_lo[...], high)
        return carry

    lax.fori_loop(0, columns // width, rows_forward, 0)

    def slabs_forward(index, carry):
        start = pl.multiple_of(index * 8, 8)
        values = []
        for slab in range(slabs):
            lanes = slice(slab * LANES, (slab + 1) * LANES)
            values.append(
                (row_part[pl.ds(start, 8), lanes], row_part[pl.ds(start + rows, 8), lanes])
            )
        for slab, (re, im) in enumerate(short_transform(values, -1)):
            if slab:
                tr, ti = twist[slab, 0], twist[slab, 1]
                re, im = re * tr - im * ti, re * ti + im * tr
            slab_part[slab, pl.ds(start, 8), :LANES] = re
            slab_part[slab, pl.ds(start, 8), LANES:] = im
        return carry

    lax.fori_loop(0, rows // 8, slabs_forward, 0)

    def lanes_both(slab, carry):
        high, low = split(slab_part[slab])
        found = mul(high, lane_hi[...]) + mul(low, lane_hi[...]) + mul(high, lane_lo[...])
        weight = mask[0, slab].astype(f32)
        re = weight * (found[:, :LANES] - real[0, slab])
        im = weight * (found[:, LANES:] - imag[0, slab])
        high, low = split(jnp.concatenate([re, im], 1))
        slab_part[slab] = mul(high, inv_hi[...]) + mul(low, inv_hi[...]) + mul(high, inv_lo[...])
        return carry

    lax.fori_loop(0, slabs, lanes_both, 0)

    def slabs_back(index, carry):
        start = pl.multiple_of(index * 8, 8)
        values = []
        for slab in range(slabs):
            re = slab_part[slab, pl.ds(start, 8), :LANES]
            im = slab_part[slab, pl.ds(start, 8), LANES:]
            if slab:
                tr, ti = twist[slab, 0], twist[slab, 1]
                re, im = re * tr + im * ti, im * tr - re * ti
            values.append((re, im))
        for slab, (re, im) in enumerate(short_transform(values, 1)):
            lanes = slice(slab * LANES, (slab + 1) * LANES)
            row_part[pl.ds(start, 8), lanes] = re
            row_part[pl.ds(start + rows, 8), lanes] = im
        return carry

    lax.fori_loop(0, rows // 8, slabs_back, 0)

    def rows_back(index, carry):
        lanes = pl.ds(pl.multiple_of(index * width, width), width)
        high, low = split(row_part[:, lanes])
        gradient = mul(back_hi[...], high) + mul(back_hi[...], low) + mul(back_lo[...], high)
        base[0, :, lanes] = sky[0, :, lanes] - primal_step * gradient
        return carry

    lax.fori_loop(0, columns // width, rows_back, 0)


def whole(array):
    return pl.BlockSpec(array.shape, lambda *index: (0,) * array.ndim)


def fidelity(sky, real, imag, mask):
    channels, rows, columns = sky.shape
    slabs = columns // LANES

    def by_slab(values):
        return values.reshape(channels, rows, LANES, slabs).transpose(0, 3, 1, 2)

    forward = row_fourier(rows)
    lane = lane_fourier(1.0 / np.sqrt(columns))
    tables = (
        *halves(forward), *halves(forward.T), *halves(lane), *halves(lane.T),
        twiddles(slabs, columns),
    )
    tables = tuple(jnp.asarray(table) for table in tables)
    image = pl.BlockSpec((1, rows, columns), lambda c: (c, 0, 0))
    slab = pl.BlockSpec((1, slabs, rows, LANES), lambda c: (c, 0, 0, 0))
    return pl.pallas_call(
        fidelity_kernel,
        out_shape=jax.ShapeDtypeStruct(sky.shape, f32),
        grid=(channels,),
        in_specs=[image, slab, slab, slab, *(whole(table) for table in tables)],
        out_specs=image,
        scratch_shapes=[
            pltpu.VMEM((2 * rows, columns), f32),
            pltpu.VMEM((slabs, rows, 2 * LANES), f32),
        ],
        compiler_params=pltpu.CompilerParams(vmem_limit_bytes=56 << 20),
        name="fidelity",
    )(sky, by_slab(real), by_slab(imag), by_slab(mask), *tables)


def prior_kernel(
    coef, base, sky, synth2, synth_lo, rowt2, rowt_lo, row2, row_lo, ana2, ana_lo,
    image, out, part_hi, part_lo, after,
):
    facets, rows, width = coef.shape[0], coef.shape[2], coef.shape[3]

    def spread(facet):
        high, low = split(coef[facet, 0])
        return mul(jnp.concatenate([high, low], 1), synth2[...]) + mul(high, synth_lo[...])

    before = spread(facets - 1)[:, width:]
    for facet in range(facets):
        both = spread(facet)
        high, low = split(both[:, :width] + before)
        before = both[:, width:]
        lanes = slice(facet * width, (facet + 1) * width)
        part_hi[:, lanes] = high
        part_lo[:, lanes] = low

    wide = 2 * width
    for index in range(facets // 2):
        lanes = slice(index * wide, (index + 1) * wide)
        high, low = part_hi[:, lanes], part_lo[:, lanes]
        step = mul(rowt2[...], jnp.concatenate([high, low], 0)) + mul(rowt_lo[...], high)
        fresh = jnp.maximum(base[0, :, lanes] - step, 0.0)
        image[0, :, lanes] = fresh
        high, low = split(2.0 * fresh - sky[0, :, lanes])
        turned = mul(row2[...], jnp.concatenate([high, low], 0)) + mul(row_lo[...], high)
        high, low = split(turned)
        for half in range(2):
            facet = 2 * index + half
            mine = slice(half * width, (half + 1) * width)
            both = mul(
                jnp.concatenate([high[:, mine], low[:, mine]], 1), ana2[...]
            ) + mul(high[:, mine], ana_lo[...])
            if facet:
                out[facet - 1, 0] = after[...] + both[:, width:]
                after[...] = both[:, :width]
            else:
                out[facets - 1, 0] = both[:, width:]
                after[...] = both[:, :width]
    out[facets - 1, 0] = after[...] + out[facets - 1, 0]


def prior(coefs, base, sky):
    channels, rows, columns = sky.shape
    facets, width = coefs.shape[0], coefs.shape[3]
    facet_table = facet_wavelet(width)
    own, other = facet_table[:, :width], facet_table[:, width:]
    synth = halves(np.concatenate([own.T, other.T], 1))
    analysis = halves(dual_step * facet_table)
    row_table = row_wavelet(rows)
    rowt = halves(primal_step * row_table.T)
    row = halves(row_table)
    tables = (
        np.concatenate([synth[0], synth[0]], 0), synth[1],
        np.concatenate([rowt[0], rowt[0]], 1), rowt[1],
        np.concatenate([row[0], row[0]], 1), row[1],
        np.concatenate([analysis[0], analysis[0]], 0), analysis[1],
    )
    tables = tuple(jnp.asarray(table) for table in tables)
    image = pl.BlockSpec((1, rows, columns), lambda c: (c, 0, 0))
    facet = pl.BlockSpec((facets, 1, rows, width), lambda c: (0, c, 0, 0))
    return pl.pallas_call(
        prior_kernel,
        out_shape=(
            jax.ShapeDtypeStruct(sky.shape, f32),
            jax.ShapeDtypeStruct(coefs.shape, f32),
        ),
        grid=(channels,),
        in_specs=[facet, image, image, *(whole(table) for table in tables)],
        out_specs=(image, facet),
        scratch_shapes=[
            pltpu.VMEM((rows, columns), bf16),
            pltpu.VMEM((rows, columns), bf16),
            pltpu.VMEM((rows, width), f32),
        ],
        compiler_params=pltpu.CompilerParams(vmem_limit_bytes=56 << 20),
        name="prior",
    )(coefs, base, sky, *tables)


def shrink_kernel(dual, change, out):
    lifted = dual[...] + change[...]
    norm = jnp.sqrt(jnp.sum(lifted * lifted, 0))
    out[...] = lifted * (1.0 / jnp.maximum(1.0, norm / ball_radius))[None]


def shrink(dual, change):
    channels, rows, width = dual.shape
    step = 8
    block = pl.BlockSpec((channels, step, width), lambda r: (0, r, 0))
    return pl.pallas_call(
        shrink_kernel,
        out_shape=jax.ShapeDtypeStruct(dual.shape, f32),
        grid=(rows // step,),
        in_specs=[block, block],
        out_specs=block,
        compiler_params=pltpu.CompilerParams(vmem_limit_bytes=56 << 20),
        name="shrink",
    )(dual, change)


def shards(sky_image, measured_real, measured_imaginary, sampling_mask, dual_field):
    channels, row_count, column_count = sky_image.shape
    facets = lax.axis_size("fac")
    width = column_count // facets
    sent = dual_field.reshape(facets, channels, row_count, width)
    coefs = lax.all_to_all(sent, "fac", split_axis=0, concat_axis=0, tiled=True)
    base = fidelity(sky_image, measured_real, measured_imaginary, sampling_mask)
    next_image, change = prior(coefs, base, sky_image)
    change = lax.all_to_all(change, "fac", split_axis=0, concat_axis=0, tiled=True)
    next_dual = shrink(dual_field, change.reshape(dual_field.shape))
    return (next_image, next_dual)


def solution(mesh):
    split_channels = P(("groups", "fac"), None, None)
    split_facets = P("groups", None, "fac")
    return jax.shard_map(
        shards,
        mesh=mesh,
        in_specs=(split_channels,) * 4 + (split_facets,),
        out_specs=(split_channels, split_facets),
        check_vma=False,
    )
```

```python
import functools

import jax
import jax.numpy as jnp
import numpy as np
from jax import lax
from jax.experimental import pallas as pl
from jax.experimental.pallas import tpu as pltpu
from jax.sharding import PartitionSpec as P

LEVELS = 4
LANES = 128

low_pass = (
    0.2303778133088964,
    0.7148465705529155,
    0.6308807679298587,
    -0.0279837694168599,
    -0.1870348117190931,
    0.0308413818355607,
    0.0328830116668852,
    -0.010597401785069,
)
high_pass = tuple(((-1) ** tap_index * low_pass[7 - tap_index] for tap_index in range(8)))
primal_step = 0.6
dual_step = 0.8
ball_radius = 12.0
f32 = jnp.float32
bf16 = jnp.bfloat16


def halves(matrix):
    high = np.asarray(matrix, np.float32).astype(bf16)
    low = (np.asarray(matrix, np.float64) - high.astype(np.float64)).astype(bf16)
    return high, low


def split(values):
    high = values.astype(bf16)
    low = (values - high.astype(f32)).astype(bf16)
    return high, low


def mul(left, right):
    return jnp.dot(left, right, preferred_element_type=f32)


def row_fourier(rows):
    grid = np.arange(rows)
    angles = 2.0 * np.pi * (np.outer(grid, grid) % rows) / rows
    return np.concatenate([np.cos(angles), -np.sin(angles)], 0) / np.sqrt(rows)


def lane_fourier(scale):
    grid = np.arange(LANES)
    angles = 2.0 * np.pi * (np.outer(grid, grid) % LANES) / LANES
    cosine, sine = np.cos(angles), np.sin(angles)
    return np.block([[cosine, -sine], [sine, cosine]]) * scale


def twiddles(slabs, columns):
    angles = 2.0 * np.pi * np.outer(np.arange(slabs), np.arange(LANES)) / columns
    table = np.stack([np.cos(angles), -np.sin(angles)], 1)
    return np.broadcast_to(table[:, :, None, :], (slabs, 2, 8, LANES)).astype(np.float32)


def row_wavelet(length):
    current = np.eye(length)
    details = []
    for level_index in range(LEVELS):
        width_now = current.shape[0]
        half_size = width_now // 2
        lower = np.zeros((half_size, width_now))
        upper = np.zeros((half_size, width_now))
        for target in range(half_size):
            for tap_index in range(8):
                lower[target, (2 * target + tap_index) % width_now] += low_pass[tap_index]
                upper[target, (2 * target + tap_index) % width_now] += high_pass[tap_index]
        details.insert(0, upper @ current)
        current = lower @ current
    return np.concatenate([current] + details, 0)


def facet_wavelet(width):
    needed = [width >> LEVELS]
    for level_index in range(LEVELS):
        needed.insert(0, 2 * (needed[0] - 1) + 8)
    current = np.eye(2 * width)
    details = []
    for level_index in range(LEVELS):
        count = needed[level_index + 1]
        lower = np.zeros((count, 2 * width))
        upper = np.zeros((count, 2 * width))
        for target in range(count):
            for tap_index in range(8):
                lower[target] += low_pass[tap_index] * current[2 * target + tap_index]
                upper[target] += high_pass[tap_index] * current[2 * target + tap_index]
        details.insert(0, upper[: width >> (level_index + 1)])
        current = lower
    matrix = np.concatenate([current[: width >> LEVELS]] + details, 0).T
    return np.concatenate([matrix[:width], matrix[width:]], 1)


def turn(value, step, length, sign):
    real, imag = value
    step = step % length
    if step == 0:
        return real, imag
    if 4 * step == length:
        return (-imag, real) if sign > 0 else (imag, -real)
    if 8 * step == length:
        root = float(np.sqrt(0.5))
        if sign > 0:
            return (real - imag) * root, (real + imag) * root
        return (real + imag) * root, (imag - real) * root
    if 8 * step == 3 * length:
        root = float(np.sqrt(0.5))
        if sign > 0:
            return (real + imag) * (-root), (real - imag) * root
        return (imag - real) * root, (real + imag) * (-root)
    cosine = float(np.cos(2.0 * np.pi * step / length))
    sine = float(sign * np.sin(2.0 * np.pi * step / length))
    return real * cosine - imag * sine, real * sine + imag * cosine


def short_transform(values, sign):
    length = len(values)
    if length == 1:
        return values
    even = short_transform(values[0::2], sign)
    odd = short_transform(values[1::2], sign)
    first, second = [], []
    for step in range(length // 2):
        real, imag = turn(odd[step], step, length, sign)
        first.append((even[step][0] + real, even[step][1] + imag))
        second.append((even[step][0] - real, even[step][1] - imag))
    return first + second


def fidelity_kernel(
    sky, real, imag, mask, row_hi, row_lo, back_hi, back_lo, lane_hi, lane_lo,
    inv_hi, inv_lo, twist, base, row_part, slab_part,
):
    rows, columns = sky.shape[1], sky.shape[2]
    slabs = columns // LANES
    width = 512

    def rows_forward(index, carry):
        lanes = pl.ds(pl.multiple_of(index * width, width), width)
        high, low = split(sky[0, :, lanes])
        row_part[:, lanes] = mul(row_hi[...], high) + mul(row_hi[...], low) + mul(row_lo[...], high)
        return carry

    lax.fori_loop(0, columns // width, rows_forward, 0)

    def slabs_forward(index, carry):
        start = pl.multiple_of(index * 8, 8)
        values = []
        for slab in range(slabs):
            lanes = slice(slab * LANES, (slab + 1) * LANES)
            values.append(
                (row_part[pl.ds(start, 8), lanes], row_part[pl.ds(start + rows, 8), lanes])
            )
        for slab, (re, im) in enumerate(short_transform(values, -1)):
            if slab:
                tr, ti = twist[slab, 0], twist[slab, 1]
                re, im = re * tr - im * ti, re * ti + im * tr
            slab_part[slab, pl.ds(start, 8), :LANES] = re
            slab_part[slab, pl.ds(start, 8), LANES:] = im
        return carry

    lax.fori_loop(0, rows // 8, slabs_forward, 0)

    group = 4

    def lanes_both(index, carry):
        pick = pl.ds(index * group, group)
        high, low = split(slab_part[pick].reshape(group * rows, 2 * LANES))
        found = mul(high, lane_hi[...]) + mul(low, lane_hi[...]) + mul(high, lane_lo[...])
        weight = mask[0, pick].reshape(group * rows, LANES).astype(f32)
        re = weight * (found[:, :LANES] - real[0, pick].reshape(group * rows, LANES))
        im = weight * (found[:, LANES:] - imag[0, pick].reshape(group * rows, LANES))
        high, low = split(jnp.concatenate([re, im], 1))
        back = mul(high, inv_hi[...]) + mul(low, inv_hi[...]) + mul(high, inv_lo[...])
        slab_part[pick] = back.reshape(group, rows, 2 * LANES)
        return carry

    lax.fori_loop(0, slabs // group, lanes_both, 0, unroll=True)

    def slabs_back(index, carry):
        start = pl.multiple_of(index * 8, 8)
        values = []
        for slab in range(slabs):
            re = slab_part[slab, pl.ds(start, 8), :LANES]
            im = slab_part[slab, pl.ds(start, 8), LANES:]
            if slab:
                tr, ti = twist[slab, 0], twist[slab, 1]
                re, im = re * tr + im * ti, im * tr - re * ti
            values.append((re, im))
        for slab, (re, im) in enumerate(short_transform(values, 1)):
            lanes = slice(slab * LANES, (slab + 1) * LANES)
            row_part[pl.ds(start, 8), lanes] = re
            row_part[pl.ds(start + rows, 8), lanes] = im
        return carry

    lax.fori_loop(0, rows // 8, slabs_back, 0)

    def rows_back(index, carry):
        lanes = pl.ds(pl.multiple_of(index * width, width), width)
        high, low = split(row_part[:, lanes])
        gradient = mul(back_hi[...], high) + mul(back_hi[...], low) + mul(back_lo[...], high)
        base[0, :, lanes] = sky[0, :, lanes] - primal_step * gradient
        return carry

    lax.fori_loop(0, columns // width, rows_back, 0)


resident = pl.BlockSpec(memory_space=pltpu.VMEM)
distant = pl.BlockSpec(memory_space=pltpu.HBM)


def remote(array):
    return pltpu.with_memory_space_constraint(array, pltpu.HBM)


def whole(array):
    return pl.BlockSpec(array.shape, lambda *index: (0,) * array.ndim)


def fidelity(sky, real, imag, mask):
    channels, rows, columns = sky.shape
    slabs = columns // LANES

    def by_slab(values):
        return values.reshape(channels, rows, LANES, slabs).transpose(0, 3, 1, 2)

    forward = row_fourier(rows)
    lane = lane_fourier(1.0 / np.sqrt(columns))
    tables = (
        *halves(forward), *halves(forward.T), *halves(lane), *halves(lane.T),
        twiddles(slabs, columns),
    )
    tables = tuple(remote(jnp.asarray(table)) for table in tables)
    image = pl.BlockSpec((1, rows, columns), lambda c: (c, 0, 0))
    slab = pl.BlockSpec((1, slabs, rows, LANES), lambda c: (c, 0, 0, 0))
    return pl.pallas_call(
        fidelity_kernel,
        out_shape=jax.ShapeDtypeStruct(sky.shape, f32),
        grid=(channels,),
        in_specs=[image, slab, slab, slab, *(whole(table) for table in tables)],
        out_specs=image,
        scratch_shapes=[
            pltpu.VMEM((2 * rows, columns), f32),
            pltpu.VMEM((slabs, rows, 2 * LANES), f32),
        ],
        compiler_params=pltpu.CompilerParams(vmem_limit_bytes=32 << 20),
        name="fidelity",
    )(remote(sky), *(remote(by_slab(values)) for values in (real, imag, mask)), *tables)


def prior_kernel(
    coef, base_far, sky_far, synth2, synth_lo, rowt2, rowt_lo, row2, row_lo, ana2, ana_lo,
    image, out, part, turned, held, base, sky, sems,
):
    facets, channels, rows, width = coef.shape
    columns = facets * width
    wide = 4 * width
    loads = []
    for channel in range(channels):
        loads.append((
            pltpu.make_async_copy(base_far.at[channel], base.at[channel], sems.at[0, channel]),
            pltpu.make_async_copy(sky_far.at[channel], sky.at[channel], sems.at[1, channel]),
        ))
        for copy in loads[-1]:
            copy.start()
    copies = []

    for channel in range(channels):

        def spread(facet):
            high, low = split(coef[facet, channel])
            return mul(jnp.concatenate([high, low], 1), synth2[...]) + mul(high, synth_lo[...])

        before = spread(facets - 1)[:, width:]
        for facet in range(facets):
            both = spread(facet)
            high, low = split(both[:, :width] + before)
            before = both[:, width:]
            lanes = slice(facet * width, (facet + 1) * width)
            part[:rows, lanes] = high
            part[rows:, lanes] = low

        for copy in loads[channel]:
            copy.wait()
        for start in range(0, columns, wide):
            lanes = slice(start, start + wide)
            both = part[:, lanes]
            step = mul(rowt2[...], both) + mul(rowt_lo[...], both[:rows])
            fresh = jnp.maximum(base[channel, :, lanes] - step, 0.0)
            base[channel, :, lanes] = fresh
            high, low = split(2.0 * fresh - sky[channel, :, lanes])
            part[:rows, lanes] = high
            part[rows:, lanes] = low

        copy = pltpu.make_async_copy(base.at[channel], image.at[channel], sems.at[2, channel])
        copy.start()
        copies.append(copy)

        for start in range(0, columns, wide):
            lanes = slice(start, start + wide)
            both = part[:, lanes]
            high, low = split(mul(row2[...], both) + mul(row_lo[...], both[:rows]))
            for index in range(wide // width):
                mine = slice(index * width, (index + 1) * width)
                turned[start // width + index, :, :width] = high[:, mine]
                turned[start // width + index, :, width:] = low[:, mine]

        before = None
        for facet in range(facets):
            both = mul(turned[facet], ana2[...]) + mul(turned[facet, :, :width], ana_lo[...])
            if facet:
                out[facet - 1, channel] = before + both[:, width:]
            else:
                held[...] = both[:, width:]
            before = both[:, :width]
        out[facets - 1, channel] = before + held[...]

    for copy in copies:
        copy.wait()


def prior(coefs, base, sky):
    channels, rows, columns = sky.shape
    facets, width = coefs.shape[0], coefs.shape[3]
    facet_table = facet_wavelet(width)
    own, other = facet_table[:, :width], facet_table[:, width:]
    synth = halves(np.concatenate([own.T, other.T], 1))
    analysis = halves(dual_step * facet_table)
    row_table = row_wavelet(rows)
    rowt = halves(primal_step * row_table.T)
    row = halves(row_table)
    tables = (
        np.concatenate([synth[0], synth[0]], 0), synth[1],
        np.concatenate([rowt[0], rowt[0]], 1), rowt[1],
        np.concatenate([row[0], row[0]], 1), row[1],
        np.concatenate([analysis[0], analysis[0]], 0), analysis[1],
    )
    tables = tuple(remote(jnp.asarray(table)) for table in tables)
    return pl.pallas_call(
        prior_kernel,
        out_shape=(
            jax.ShapeDtypeStruct(sky.shape, f32),
            jax.ShapeDtypeStruct(coefs.shape, f32),
        ),
        in_specs=[resident, distant, distant, *(whole(table) for table in tables)],
        out_specs=(distant, resident),
        scratch_shapes=[
            pltpu.VMEM((2 * rows, columns), bf16),
            pltpu.VMEM((facets, rows, 2 * width), bf16),
            pltpu.VMEM((rows, width), f32),
            pltpu.VMEM(sky.shape, f32),
            pltpu.VMEM(sky.shape, f32),
            pltpu.SemaphoreType.DMA((3, channels)),
        ],
        compiler_params=pltpu.CompilerParams(vmem_limit_bytes=16 << 20),
        name="prior",
    )(coefs, remote(base), remote(sky), *tables)


def shrink_kernel(dual, change, out):
    lifted = dual[...] + change[...]
    norm = jnp.sqrt(jnp.sum(lifted * lifted, 0))
    out[...] = lifted * (1.0 / jnp.maximum(1.0, norm / ball_radius))[None]


def shrink(dual, change):
    channels, rows, width = dual.shape
    step = rows // 2
    block = pl.BlockSpec((channels, step, width), lambda r: (0, r, 0))
    return pl.pallas_call(
        shrink_kernel,
        out_shape=jax.ShapeDtypeStruct(dual.shape, f32),
        grid=(rows // step,),
        in_specs=[block, block],
        out_specs=block,
        compiler_params=pltpu.CompilerParams(vmem_limit_bytes=12 << 20),
        name="shrink",
    )(dual, change)


def shards(sky_image, measured_real, measured_imaginary, sampling_mask, dual_field):
    channels, row_count, column_count = sky_image.shape
    facets = lax.axis_size("fac")
    width = column_count // facets
    sent = dual_field.reshape(facets, channels, row_count, width)
    coefs = lax.all_to_all(sent, "fac", split_axis=0, concat_axis=0, tiled=True)
    base = fidelity(sky_image, measured_real, measured_imaginary, sampling_mask)
    next_image, change = prior(coefs, base, sky_image)
    change = lax.all_to_all(change, "fac", split_axis=0, concat_axis=0, tiled=True)
    next_dual = shrink(dual_field, change.reshape(dual_field.shape))
    return (next_image, next_dual)


def solution(mesh):
    split_channels = P(("groups", "fac"), None, None)
    split_facets = P("groups", None, "fac")
    return jax.shard_map(
        shards,
        mesh=mesh,
        in_specs=(split_channels,) * 4 + (split_facets,),
        out_specs=(split_channels, split_facets),
        check_vma=False,
    )
```

```python
import functools

import jax
import jax.numpy as jnp
import numpy as np
from jax import lax
from jax.experimental import pallas as pl
from jax.experimental.pallas import tpu as pltpu
from jax.sharding import PartitionSpec as P

LEVELS = 4
LANES = 128

low_pass = (
    0.2303778133088964,
    0.7148465705529155,
    0.6308807679298587,
    -0.0279837694168599,
    -0.1870348117190931,
    0.0308413818355607,
    0.0328830116668852,
    -0.010597401785069,
)
high_pass = tuple(((-1) ** tap_index * low_pass[7 - tap_index] for tap_index in range(8)))
primal_step = 0.6
dual_step = 0.8
ball_radius = 12.0
f32 = jnp.float32
bf16 = jnp.bfloat16


def halves(matrix):
    high = np.asarray(matrix, np.float32).astype(bf16)
    low = (np.asarray(matrix, np.float64) - high.astype(np.float64)).astype(bf16)
    return high, low


def split(values):
    high = values.astype(bf16)
    low = (values - high.astype(f32)).astype(bf16)
    return high, low


def mul(left, right):
    return jnp.dot(left, right, preferred_element_type=f32)


def row_fourier(rows):
    grid = np.arange(rows)
    angles = 2.0 * np.pi * (np.outer(grid, grid) % rows) / rows
    return np.concatenate([np.cos(angles), -np.sin(angles)], 0) / np.sqrt(rows)


def lane_fourier(scale):
    grid = np.arange(LANES)
    angles = 2.0 * np.pi * (np.outer(grid, grid) % LANES) / LANES
    cosine, sine = np.cos(angles), np.sin(angles)
    return np.block([[cosine, -sine], [sine, cosine]]) * scale


def twiddles(slabs, columns):
    angles = 2.0 * np.pi * np.outer(np.arange(slabs), np.arange(LANES)) / columns
    table = np.stack([np.cos(angles), -np.sin(angles)], 1)
    return np.broadcast_to(table[:, :, None, :], (slabs, 2, 8, LANES)).astype(np.float32)


def row_wavelet(length):
    current = np.eye(length)
    details = []
    for level_index in range(LEVELS):
        width_now = current.shape[0]
        half_size = width_now // 2
        lower = np.zeros((half_size, width_now))
        upper = np.zeros((half_size, width_now))
        for target in range(half_size):
            for tap_index in range(8):
                lower[target, (2 * target + tap_index) % width_now] += low_pass[tap_index]
                upper[target, (2 * target + tap_index) % width_now] += high_pass[tap_index]
        details.insert(0, upper @ current)
        current = lower @ current
    return np.concatenate([current] + details, 0)


def facet_wavelet(width):
    needed = [width >> LEVELS]
    for level_index in range(LEVELS):
        needed.insert(0, 2 * (needed[0] - 1) + 8)
    current = np.eye(2 * width)
    details = []
    for level_index in range(LEVELS):
        count = needed[level_index + 1]
        lower = np.zeros((count, 2 * width))
        upper = np.zeros((count, 2 * width))
        for target in range(count):
            for tap_index in range(8):
                lower[target] += low_pass[tap_index] * current[2 * target + tap_index]
                upper[target] += high_pass[tap_index] * current[2 * target + tap_index]
        details.insert(0, upper[: width >> (level_index + 1)])
        current = lower
    matrix = np.concatenate([current[: width >> LEVELS]] + details, 0).T
    return np.concatenate([matrix[:width], matrix[width:]], 1)


def turn(value, step, length, sign):
    real, imag = value
    step = step % length
    if step == 0:
        return real, imag
    if 4 * step == length:
        return (-imag, real) if sign > 0 else (imag, -real)
    if 8 * step == length:
        root = float(np.sqrt(0.5))
        if sign > 0:
            return (real - imag) * root, (real + imag) * root
        return (real + imag) * root, (imag - real) * root
    if 8 * step == 3 * length:
        root = float(np.sqrt(0.5))
        if sign > 0:
            return (real + imag) * (-root), (real - imag) * root
        return (imag - real) * root, (real + imag) * (-root)
    cosine = float(np.cos(2.0 * np.pi * step / length))
    sine = float(sign * np.sin(2.0 * np.pi * step / length))
    return real * cosine - imag * sine, real * sine + imag * cosine


def short_transform(values, sign):
    length = len(values)
    if length == 1:
        return values
    even = short_transform(values[0::2], sign)
    odd = short_transform(values[1::2], sign)
    first, second = [], []
    for step in range(length // 2):
        real, imag = turn(odd[step], step, length, sign)
        first.append((even[step][0] + real, even[step][1] + imag))
        second.append((even[step][0] - real, even[step][1] - imag))
    return first + second


def fidelity_kernel(
    sky, real, imag, mask, row_hi, row_lo, back_hi, back_lo, lane_hi, lane_lo,
    inv_hi, inv_lo, twist, base, row_part, slab_part,
):
    rows, columns = sky.shape[1], sky.shape[2]
    slabs = columns // LANES
    width = 512

    def rows_forward(index, carry):
        lanes = pl.ds(pl.multiple_of(index * width, width), width)
        high, low = split(sky[0, :, lanes])
        row_part[:, lanes] = mul(row_hi[...], high) + mul(row_hi[...], low) + mul(row_lo[...], high)
        return carry

    lax.fori_loop(0, columns // width, rows_forward, 0)

    def slabs_forward(index, carry):
        start = pl.multiple_of(index * 8, 8)
        values = []
        for slab in range(slabs):
            lanes = slice(slab * LANES, (slab + 1) * LANES)
            values.append(
                (row_part[pl.ds(start, 8), lanes], row_part[pl.ds(start + rows, 8), lanes])
            )
        for slab, (re, im) in enumerate(short_transform(values, -1)):
            if slab:
                tr, ti = twist[slab, 0], twist[slab, 1]
                re, im = re * tr - im * ti, re * ti + im * tr
            slab_part[slab, pl.ds(start, 8), :LANES] = re
            slab_part[slab, pl.ds(start, 8), LANES:] = im
        return carry

    lax.fori_loop(0, rows // 8, slabs_forward, 0)

    group = 4

    def lanes_both(index, carry):
        pick = pl.ds(index * group, group)
        high, low = split(slab_part[pick].reshape(group * rows, 2 * LANES))
        found = mul(high, lane_hi[...]) + mul(low, lane_hi[...]) + mul(high, lane_lo[...])
        weight = mask[0, pick].reshape(group * rows, LANES).astype(f32)
        re = weight * (found[:, :LANES] - real[0, pick].reshape(group * rows, LANES))
        im = weight * (found[:, LANES:] - imag[0, pick].reshape(group * rows, LANES))
        high, low = split(jnp.concatenate([re, im], 1))
        back = mul(high, inv_hi[...]) + mul(low, inv_hi[...]) + mul(high, inv_lo[...])
        slab_part[pick] = back.reshape(group, rows, 2 * LANES)
        return carry

    lax.fori_loop(0, slabs // group, lanes_both, 0, unroll=True)

    def slabs_back(index, carry):
        start = pl.multiple_of(index * 8, 8)
        values = []
        for slab in range(slabs):
            re = slab_part[slab, pl.ds(start, 8), :LANES]
            im = slab_part[slab, pl.ds(start, 8), LANES:]
            if slab:
                tr, ti = twist[slab, 0], twist[slab, 1]
                re, im = re * tr + im * ti, im * tr - re * ti
            values.append((re, im))
        for slab, (re, im) in enumerate(short_transform(values, 1)):
            lanes = slice(slab * LANES, (slab + 1) * LANES)
            row_part[pl.ds(start, 8), lanes] = re
            row_part[pl.ds(start + rows, 8), lanes] = im
        return carry

    lax.fori_loop(0, rows // 8, slabs_back, 0)

    def rows_back(index, carry):
        lanes = pl.ds(pl.multiple_of(index * width, width), width)
        high, low = split(row_part[:, lanes])
        gradient = mul(back_hi[...], high) + mul(back_hi[...], low) + mul(back_lo[...], high)
        base[0, :, lanes] = sky[0, :, lanes] - primal_step * gradient
        return carry

    lax.fori_loop(0, columns // width, rows_back, 0)


resident = pl.BlockSpec(memory_space=pltpu.VMEM)
distant = pl.BlockSpec(memory_space=pltpu.HBM)


def remote(array):
    return pltpu.with_memory_space_constraint(array, pltpu.HBM)


def whole(array):
    return pl.BlockSpec(array.shape, lambda *index: (0,) * array.ndim)


def fidelity(sky, real, imag, mask):
    channels, rows, columns = sky.shape
    slabs = columns // LANES

    def by_slab(values):
        return values.reshape(channels, rows, LANES, slabs).transpose(0, 3, 1, 2)

    forward = row_fourier(rows)
    lane = lane_fourier(1.0 / np.sqrt(columns))
    tables = (
        *halves(forward), *halves(forward.T), *halves(lane), *halves(lane.T),
        twiddles(slabs, columns),
    )
    tables = tuple(remote(jnp.asarray(table)) for table in tables)
    image = pl.BlockSpec((1, rows, columns), lambda c: (c, 0, 0))
    slab = pl.BlockSpec((1, slabs, rows, LANES), lambda c: (c, 0, 0, 0))
    return pl.pallas_call(
        fidelity_kernel,
        out_shape=jax.ShapeDtypeStruct(sky.shape, f32),
        grid=(channels,),
        in_specs=[image, slab, slab, slab, *(whole(table) for table in tables)],
        out_specs=image,
        scratch_shapes=[
            pltpu.VMEM((2 * rows, columns), f32),
            pltpu.VMEM((slabs, rows, 2 * LANES), f32),
        ],
        compiler_params=pltpu.CompilerParams(vmem_limit_bytes=32 << 20),
        name="fidelity",
    )(remote(sky), *(remote(by_slab(values)) for values in (real, imag, mask)), *tables)


def prior_kernel(*refs):
    coef, base_far, sky_far = refs[:3]
    tables_far, tables = refs[3:11], refs[13:21]
    image, out = refs[11:13]
    part, turned, held, base, sky, sems, table_sems = refs[21:]
    synth2, synth_lo, rowt2, rowt_lo, row2, row_lo, ana2, ana_lo = tables
    facets, channels, rows, width = coef.shape
    columns = facets * width
    wide = 4 * width
    batch = 4

    fetches = [
        pltpu.make_async_copy(tables_far[index], tables[index], table_sems.at[index])
        for index in range(len(tables))
    ]
    loads = [
        (
            pltpu.make_async_copy(base_far.at[channel], base.at[channel], sems.at[0, channel]),
            pltpu.make_async_copy(sky_far.at[channel], sky.at[channel], sems.at[1, channel]),
        )
        for channel in range(channels)
    ]
    for copy in (*fetches[:2], *loads[0], *fetches[2:]):
        copy.start()
    copies = []

    for copy in fetches[:2]:
        copy.wait()
    for channel in range(channels):

        before = None
        for first in range(0, facets, batch):
            high, low = split(coef[first : first + batch, channel].reshape(batch * rows, width))
            both = mul(jnp.concatenate([high, low], 1), synth2[...]) + mul(high, synth_lo[...])
            for index in range(batch):
                facet = first + index
                mine = both[index * rows : (index + 1) * rows]
                if facet:
                    high, low = split(mine[:, :width] + before)
                    lanes = slice(facet * width, (facet + 1) * width)
                    part[channel, :rows, lanes] = high
                    part[channel, rows:, lanes] = low
                else:
                    held[...] = mine[:, :width]
                before = mine[:, width:]
        high, low = split(held[...] + before)
        part[channel, :rows, :width] = high
        part[channel, rows:, :width] = low

    for copy in fetches[2:4]:
        copy.wait()
    for channel in range(channels):
        for copy in loads[channel]:
            copy.wait()
        if channel + 1 < channels:
            for copy in loads[channel + 1]:
                copy.start()
        for start in range(0, columns, wide):
            lanes = slice(start, start + wide)
            both = part[channel, :, lanes]
            step = mul(rowt2[...], both) + mul(rowt_lo[...], both[:rows])
            fresh = jnp.maximum(base[channel, :, lanes] - step, 0.0)
            base[channel, :, lanes] = fresh
            high, low = split(2.0 * fresh - sky[channel, :, lanes])
            part[channel, :rows, lanes] = high
            part[channel, rows:, lanes] = low
        copy = pltpu.make_async_copy(base.at[channel], image.at[channel], sems.at[2, channel])
        copy.start()
        copies.append(copy)

        if channel == 0:
            for copy in fetches[4:]:
                copy.wait()
        for start in range(0, columns, wide):
            lanes = slice(start, start + wide)
            both = part[channel, :, lanes]
            high, low = split(mul(row2[...], both) + mul(row_lo[...], both[:rows]))
            for index in range(wide // width):
                mine = slice(index * width, (index + 1) * width)
                turned[channel, start // width + index, :, :width] = high[:, mine]
                turned[channel, start // width + index, :, width:] = low[:, mine]

        before = None
        for first in range(0, facets, batch):
            values = turned[channel, first : first + batch].reshape(batch * rows, 2 * width)
            both = mul(values, ana2[...]) + mul(values[:, :width], ana_lo[...])
            for index in range(batch):
                facet = first + index
                mine = both[index * rows : (index + 1) * rows]
                if facet:
                    out[facet - 1, channel] = before + mine[:, width:]
                else:
                    held[...] = mine[:, width:]
                before = mine[:, :width]
        out[facets - 1, channel] = before + held[...]

    for copy in copies:
        copy.wait()


def prior(coefs, base, sky):
    channels, rows, columns = sky.shape
    facets, width = coefs.shape[0], coefs.shape[3]
    facet_table = facet_wavelet(width)
    own, other = facet_table[:, :width], facet_table[:, width:]
    synth = halves(np.concatenate([own.T, other.T], 1))
    analysis = halves(dual_step * facet_table)
    row_table = row_wavelet(rows)
    rowt = halves(primal_step * row_table.T)
    row = halves(row_table)
    tables = (
        np.concatenate([synth[0], synth[0]], 0), synth[1],
        np.concatenate([rowt[0], rowt[0]], 1), rowt[1],
        np.concatenate([row[0], row[0]], 1), row[1],
        np.concatenate([analysis[0], analysis[0]], 0), analysis[1],
    )
    tables = tuple(remote(jnp.asarray(table)) for table in tables)
    return pl.pallas_call(
        prior_kernel,
        out_shape=(
            jax.ShapeDtypeStruct(sky.shape, f32),
            jax.ShapeDtypeStruct(coefs.shape, f32),
        ),
        in_specs=[resident, distant, distant, *(distant for table in tables)],
        out_specs=(distant, resident),
        scratch_shapes=[
            *(pltpu.VMEM(table.shape, bf16) for table in tables),
            pltpu.VMEM((channels, 2 * rows, columns), bf16),
            pltpu.VMEM((channels, facets, rows, 2 * width), bf16),
            pltpu.VMEM((rows, width), f32),
            pltpu.VMEM(sky.shape, f32),
            pltpu.VMEM(sky.shape, f32),
            pltpu.SemaphoreType.DMA((3, channels)),
            pltpu.SemaphoreType.DMA((len(tables),)),
        ],
        compiler_params=pltpu.CompilerParams(vmem_limit_bytes=20 << 20),
        name="prior",
    )(coefs, remote(base), remote(sky), *tables)


def shrink_kernel(dual, change, out_far, out, sems):
    channels = dual.shape[0]
    some = channels // sems.shape[0]
    total = 0.0
    for channel in range(channels):
        lifted = dual[channel] + change[channel]
        total = total + lifted * lifted
    scale = 1.0 / jnp.maximum(1.0, jnp.sqrt(total) / ball_radius)
    copies = []
    for first in range(0, channels, some):
        for channel in range(first, first + some):
            out[channel] = (dual[channel] + change[channel]) * scale
        pick = pl.ds(first, some)
        copy = pltpu.make_async_copy(out.at[pick], out_far.at[pick], sems.at[first // some])
        copy.start()
        copies.append(copy)
    for copy in copies:
        copy.wait()


def shrink(dual, change):
    return pl.pallas_call(
        shrink_kernel,
        out_shape=jax.ShapeDtypeStruct(dual.shape, f32),
        in_specs=[resident, resident],
        out_specs=distant,
        scratch_shapes=[pltpu.VMEM(dual.shape, f32), pltpu.SemaphoreType.DMA((8,))],
        compiler_params=pltpu.CompilerParams(vmem_limit_bytes=6 << 20),
        name="shrink",
    )(dual, change)


def shards(sky_image, measured_real, measured_imaginary, sampling_mask, dual_field):
    channels, row_count, column_count = sky_image.shape
    facets = lax.axis_size("fac")
    width = column_count // facets
    sent = dual_field.reshape(facets, channels, row_count, width)
    coefs = lax.all_to_all(sent, "fac", split_axis=0, concat_axis=0, tiled=True)
    base = fidelity(sky_image, measured_real, measured_imaginary, sampling_mask)
    next_image, change = prior(coefs, base, sky_image)
    change = lax.all_to_all(change, "fac", split_axis=0, concat_axis=0, tiled=True)
    next_dual = shrink(dual_field, change.reshape(dual_field.shape))
    return (next_image, next_dual)


def solution(mesh):
    split_channels = P(("groups", "fac"), None, None)
    split_facets = P("groups", None, "fac")
    return jax.shard_map(
        shards,
        mesh=mesh,
        in_specs=(split_channels,) * 4 + (split_facets,),
        out_specs=(split_channels, split_facets),
        check_vma=False,
    )
```

```python
import functools

import jax
import jax.numpy as jnp
import numpy as np
from jax import lax
from jax.experimental import pallas as pl
from jax.experimental.pallas import tpu as pltpu
from jax.sharding import PartitionSpec as P

LEVELS = 4
LANES = 128

low_pass = (
    0.2303778133088964,
    0.7148465705529155,
    0.6308807679298587,
    -0.0279837694168599,
    -0.1870348117190931,
    0.0308413818355607,
    0.0328830116668852,
    -0.010597401785069,
)
high_pass = tuple(((-1) ** tap_index * low_pass[7 - tap_index] for tap_index in range(8)))
primal_step = 0.6
dual_step = 0.8
ball_radius = 12.0
f32 = jnp.float32
bf16 = jnp.bfloat16


def halves(matrix):
    high = np.asarray(matrix, np.float32).astype(bf16)
    low = (np.asarray(matrix, np.float64) - high.astype(np.float64)).astype(bf16)
    return high, low


def split(values):
    high = values.astype(bf16)
    low = (values - high.astype(f32)).astype(bf16)
    return high, low


def mul(left, right):
    return jnp.dot(left, right, preferred_element_type=f32)


def row_fourier(rows):
    grid = np.arange(rows)
    angles = 2.0 * np.pi * (np.outer(grid, grid) % rows) / rows
    return np.concatenate([np.cos(angles), -np.sin(angles)], 0) / np.sqrt(rows)


def lane_fourier(scale):
    grid = np.arange(LANES)
    angles = 2.0 * np.pi * (np.outer(grid, grid) % LANES) / LANES
    cosine, sine = np.cos(angles), np.sin(angles)
    return np.block([[cosine, -sine], [sine, cosine]]) * scale


def twiddles(slabs, columns):
    angles = 2.0 * np.pi * np.outer(np.arange(slabs), np.arange(LANES)) / columns
    table = np.stack([np.cos(angles), -np.sin(angles)], 1)
    return np.broadcast_to(table[:, :, None, :], (slabs, 2, 8, LANES)).astype(np.float32)


def row_wavelet(length):
    current = np.eye(length)
    details = []
    for level_index in range(LEVELS):
        width_now = current.shape[0]
        half_size = width_now // 2
        lower = np.zeros((half_size, width_now))
        upper = np.zeros((half_size, width_now))
        for target in range(half_size):
            for tap_index in range(8):
                lower[target, (2 * target + tap_index) % width_now] += low_pass[tap_index]
                upper[target, (2 * target + tap_index) % width_now] += high_pass[tap_index]
        details.insert(0, upper @ current)
        current = lower @ current
    return np.concatenate([current] + details, 0)


def facet_wavelet(width):
    needed = [width >> LEVELS]
    for level_index in range(LEVELS):
        needed.insert(0, 2 * (needed[0] - 1) + 8)
    current = np.eye(2 * width)
    details = []
    for level_index in range(LEVELS):
        count = needed[level_index + 1]
        lower = np.zeros((count, 2 * width))
        upper = np.zeros((count, 2 * width))
        for target in range(count):
            for tap_index in range(8):
                lower[target] += low_pass[tap_index] * current[2 * target + tap_index]
                upper[target] += high_pass[tap_index] * current[2 * target + tap_index]
        details.insert(0, upper[: width >> (level_index + 1)])
        current = lower
    matrix = np.concatenate([current[: width >> LEVELS]] + details, 0).T
    return np.concatenate([matrix[:width], matrix[width:]], 1)


def turn(value, step, length, sign):
    real, imag = value
    step = step % length
    if step == 0:
        return real, imag
    if 4 * step == length:
        return (-imag, real) if sign > 0 else (imag, -real)
    if 8 * step == length:
        root = float(np.sqrt(0.5))
        if sign > 0:
            return (real - imag) * root, (real + imag) * root
        return (real + imag) * root, (imag - real) * root
    if 8 * step == 3 * length:
        root = float(np.sqrt(0.5))
        if sign > 0:
            return (real + imag) * (-root), (real - imag) * root
        return (imag - real) * root, (real + imag) * (-root)
    cosine = float(np.cos(2.0 * np.pi * step / length))
    sine = float(sign * np.sin(2.0 * np.pi * step / length))
    return real * cosine - imag * sine, real * sine + imag * cosine


def short_transform(values, sign):
    length = len(values)
    if length == 1:
        return values
    even = short_transform(values[0::2], sign)
    odd = short_transform(values[1::2], sign)
    first, second = [], []
    for step in range(length // 2):
        real, imag = turn(odd[step], step, length, sign)
        first.append((even[step][0] + real, even[step][1] + imag))
        second.append((even[step][0] - real, even[step][1] - imag))
    return first + second


def fidelity_kernel(
    sky, real, imag, mask, row_hi, row_lo, back_hi, back_lo, lane_hi, lane_lo,
    inv_hi, inv_lo, twist, early_far, base, early, row_part, slab_part, sem,
):
    rows, columns = sky.shape[1], sky.shape[2]
    slabs = columns // LANES
    width = 512

    @pl.when(pl.program_id(0) == 0)
    def fetch():
        copy = pltpu.make_async_copy(early_far, early, sem)
        copy.start()
        copy.wait()


    def rows_forward(index, carry):
        lanes = pl.ds(pl.multiple_of(index * width, width), width)
        high, low = split(sky[0, :, lanes])
        row_part[:, lanes] = mul(row_hi[...], high) + mul(row_hi[...], low) + mul(row_lo[...], high)
        return carry

    lax.fori_loop(0, columns // width, rows_forward, 0)

    def slabs_forward(index, carry):
        start = pl.multiple_of(index * 8, 8)
        values = []
        for slab in range(slabs):
            lanes = slice(slab * LANES, (slab + 1) * LANES)
            values.append(
                (row_part[pl.ds(start, 8), lanes], row_part[pl.ds(start + rows, 8), lanes])
            )
        for slab, (re, im) in enumerate(short_transform(values, -1)):
            if slab:
                tr, ti = twist[slab, 0], twist[slab, 1]
                re, im = re * tr - im * ti, re * ti + im * tr
            slab_part[slab, pl.ds(start, 8), :LANES] = re
            slab_part[slab, pl.ds(start, 8), LANES:] = im
        return carry

    lax.fori_loop(0, rows // 8, slabs_forward, 0)

    group = 4

    def lanes_both(index, carry):
        pick = pl.ds(index * group, group)
        high, low = split(slab_part[pick].reshape(group * rows, 2 * LANES))
        found = mul(high, lane_hi[...]) + mul(low, lane_hi[...]) + mul(high, lane_lo[...])
        weight = mask[0, pick].reshape(group * rows, LANES).astype(f32)
        re = weight * (found[:, :LANES] - real[0, pick].reshape(group * rows, LANES))
        im = weight * (found[:, LANES:] - imag[0, pick].reshape(group * rows, LANES))
        high, low = split(jnp.concatenate([re, im], 1))
        back = mul(high, inv_hi[...]) + mul(low, inv_hi[...]) + mul(high, inv_lo[...])
        slab_part[pick] = back.reshape(group, rows, 2 * LANES)
        return carry

    lax.fori_loop(0, slabs // group, lanes_both, 0, unroll=True)

    def slabs_back(index, carry):
        start = pl.multiple_of(index * 8, 8)
        values = []
        for slab in range(slabs):
            re = slab_part[slab, pl.ds(start, 8), :LANES]
            im = slab_part[slab, pl.ds(start, 8), LANES:]
            if slab:
                tr, ti = twist[slab, 0], twist[slab, 1]
                re, im = re * tr + im * ti, im * tr - re * ti
            values.append((re, im))
        for slab, (re, im) in enumerate(short_transform(values, 1)):
            lanes = slice(slab * LANES, (slab + 1) * LANES)
            row_part[pl.ds(start, 8), lanes] = re
            row_part[pl.ds(start + rows, 8), lanes] = im
        return carry

    lax.fori_loop(0, rows // 8, slabs_back, 0)

    def rows_back(index, carry):
        lanes = pl.ds(pl.multiple_of(index * width, width), width)
        high, low = split(row_part[:, lanes])
        gradient = mul(back_hi[...], high) + mul(back_hi[...], low) + mul(back_lo[...], high)
        base[0, :, lanes] = sky[0, :, lanes] - primal_step * gradient
        return carry

    lax.fori_loop(0, columns // width, rows_back, 0)


resident = pl.BlockSpec(memory_space=pltpu.VMEM)
distant = pl.BlockSpec(memory_space=pltpu.HBM)


def remote(array):
    return pltpu.with_memory_space_constraint(array, pltpu.HBM)


def whole(array):
    return pl.BlockSpec(array.shape, lambda *index: (0,) * array.ndim)


def fidelity(sky, real, imag, mask, early):
    channels, rows, columns = sky.shape
    slabs = columns // LANES

    def by_slab(values):
        return values.reshape(channels, rows, LANES, slabs).transpose(0, 3, 1, 2)

    forward = row_fourier(rows)
    lane = lane_fourier(1.0 / np.sqrt(columns))
    tables = (
        *halves(forward), *halves(forward.T), *halves(lane), *halves(lane.T),
        twiddles(slabs, columns),
    )
    tables = tuple(remote(jnp.asarray(table)) for table in tables)
    image = pl.BlockSpec((1, rows, columns), lambda c: (c, 0, 0))
    slab = pl.BlockSpec((1, slabs, rows, LANES), lambda c: (c, 0, 0, 0))
    return pl.pallas_call(
        fidelity_kernel,
        out_shape=(
            jax.ShapeDtypeStruct(sky.shape, f32),
            jax.ShapeDtypeStruct(early.shape, early.dtype),
        ),
        grid=(channels,),
        in_specs=[image, slab, slab, slab, *(whole(table) for table in tables), distant],
        out_specs=(image, resident),
        scratch_shapes=[
            pltpu.VMEM((2 * rows, columns), f32),
            pltpu.VMEM((slabs, rows, 2 * LANES), f32),
            pltpu.SemaphoreType.DMA,
        ],
        compiler_params=pltpu.CompilerParams(vmem_limit_bytes=32 << 20),
        name="fidelity",
    )(remote(sky), *(remote(by_slab(values)) for values in (real, imag, mask)), *tables, remote(early))


def prior_kernel(*refs):
    coef, base_far, sky_far, kept = refs[:4]
    tables_far, tables = refs[4:10], refs[12:18]
    image, out = refs[10:12]
    part, turned, held, base, sky, sems, table_sems, synth = refs[18:]
    rowt2, rowt_lo, row2, row_lo, ana2, ana_lo = tables
    facets, channels, rows, width = coef.shape
    synth2, synth_lo = synth.at[: 2 * width], synth.at[2 * width :]
    columns = facets * width
    wide = 4 * width
    batch = 4

    first_table = pltpu.make_async_copy(kept, synth, table_sems.at[len(tables)])
    first_table.start()
    fetches = [
        pltpu.make_async_copy(tables_far[index], tables[index], table_sems.at[index])
        for index in range(len(tables))
    ]
    loads = [
        (
            pltpu.make_async_copy(base_far.at[channel], base.at[channel], sems.at[0, channel]),
            pltpu.make_async_copy(sky_far.at[channel], sky.at[channel], sems.at[1, channel]),
        )
        for channel in range(channels)
    ]
    for copy in (*fetches[:2], *loads[0], *fetches[2:], *loads[1]):
        copy.start()
    copies = []

    first_table.wait()
    for channel in range(channels):

        before = None
        for first in range(0, facets, batch):
            high, low = split(coef[first : first + batch, channel].reshape(batch * rows, width))
            both = mul(jnp.concatenate([high, low], 1), synth2[...]) + mul(high, synth_lo[...])
            for index in range(batch):
                facet = first + index
                mine = both[index * rows : (index + 1) * rows]
                if facet:
                    high, low = split(mine[:, :width] + before)
                    lanes = slice(facet * width, (facet + 1) * width)
                    part[channel, :rows, lanes] = high
                    part[channel, rows:, lanes] = low
                else:
                    held[...] = mine[:, :width]
                before = mine[:, width:]
        high, low = split(held[...] + before)
        part[channel, :rows, :width] = high
        part[channel, rows:, :width] = low

    for copy in fetches[:2]:
        copy.wait()
    for channel in range(channels):
        for copy in loads[channel]:
            copy.wait()
        for start in range(0, columns, wide):
            lanes = slice(start, start + wide)
            both = part[channel, :, lanes]
            step = mul(rowt2[...], both) + mul(rowt_lo[...], both[:rows])
            fresh = jnp.maximum(base[channel, :, lanes] - step, 0.0)
            base[channel, :, lanes] = fresh
            high, low = split(2.0 * fresh - sky[channel, :, lanes])
            part[channel, :rows, lanes] = high
            part[channel, rows:, lanes] = low
        copy = pltpu.make_async_copy(base.at[channel], image.at[channel], sems.at[2, channel])
        copy.start()
        copies.append(copy)

        if channel == 0:
            for copy in fetches[2:]:
                copy.wait()
        for start in range(0, columns, wide):
            lanes = slice(start, start + wide)
            both = part[channel, :, lanes]
            high, low = split(mul(row2[...], both) + mul(row_lo[...], both[:rows]))
            for index in range(wide // width):
                mine = slice(index * width, (index + 1) * width)
                turned[channel, start // width + index, :, :width] = high[:, mine]
                turned[channel, start // width + index, :, width:] = low[:, mine]

        before = None
        for first in range(0, facets, batch):
            values = turned[channel, first : first + batch].reshape(batch * rows, 2 * width)
            both = mul(values, ana2[...]) + mul(values[:, :width], ana_lo[...])
            for index in range(batch):
                facet = first + index
                mine = both[index * rows : (index + 1) * rows]
                if facet:
                    out[facet - 1, channel] = before + mine[:, width:]
                else:
                    held[...] = mine[:, width:]
                before = mine[:, :width]
        out[facets - 1, channel] = before + held[...]

    for copy in copies:
        copy.wait()


def synthesis_table(width):
    facet_table = facet_wavelet(width)
    own, other = facet_table[:, :width], facet_table[:, width:]
    high, low = halves(np.concatenate([own.T, other.T], 1))
    return jnp.asarray(np.concatenate([high, high, low], 0))


def prior(coefs, base, sky, synth):
    channels, rows, columns = sky.shape
    facets, width = coefs.shape[0], coefs.shape[3]
    facet_table = facet_wavelet(width)
    analysis = halves(dual_step * facet_table)
    row_table = row_wavelet(rows)
    rowt = halves(primal_step * row_table.T)
    row = halves(row_table)
    tables = (
        np.concatenate([rowt[0], rowt[0]], 1), rowt[1],
        np.concatenate([row[0], row[0]], 1), row[1],
        np.concatenate([analysis[0], analysis[0]], 0), analysis[1],
    )
    tables = tuple(remote(jnp.asarray(table)) for table in tables)
    return pl.pallas_call(
        prior_kernel,
        out_shape=(
            jax.ShapeDtypeStruct(sky.shape, f32),
            jax.ShapeDtypeStruct(coefs.shape, f32),
        ),
        in_specs=[resident, distant, distant, resident, *(distant for table in tables)],
        out_specs=(distant, resident),
        scratch_shapes=[
            *(pltpu.VMEM(table.shape, bf16) for table in tables),
            pltpu.VMEM((channels, 2 * rows, columns), bf16),
            pltpu.VMEM((channels, facets, rows, 2 * width), bf16),
            pltpu.VMEM((rows, width), f32),
            pltpu.VMEM(sky.shape, f32),
            pltpu.VMEM(sky.shape, f32),
            pltpu.SemaphoreType.DMA((3, channels)),
            pltpu.SemaphoreType.DMA((len(tables) + 1,)),
            pltpu.VMEM(synth.shape, bf16),
        ],
        compiler_params=pltpu.CompilerParams(vmem_limit_bytes=20 << 20),
        name="prior",
    )(coefs, remote(base), remote(sky), synth, *tables)


def shrink_kernel(dual, change, out_far, out, sems):
    channels = dual.shape[0]
    some = channels // sems.shape[0]
    total = 0.0
    for channel in range(channels):
        lifted = dual[channel] + change[channel]
        total = total + lifted * lifted
    scale = 1.0 / jnp.maximum(1.0, jnp.sqrt(total) / ball_radius)
    copies = []
    for first in range(0, channels, some):
        for channel in range(first, first + some):
            out[channel] = (dual[channel] + change[channel]) * scale
        pick = pl.ds(first, some)
        copy = pltpu.make_async_copy(out.at[pick], out_far.at[pick], sems.at[first // some])
        copy.start()
        copies.append(copy)
    for copy in copies:
        copy.wait()


def shrink(dual, change):
    return pl.pallas_call(
        shrink_kernel,
        out_shape=jax.ShapeDtypeStruct(dual.shape, f32),
        in_specs=[resident, resident],
        out_specs=distant,
        scratch_shapes=[pltpu.VMEM(dual.shape, f32), pltpu.SemaphoreType.DMA((8,))],
        compiler_params=pltpu.CompilerParams(vmem_limit_bytes=6 << 20),
        name="shrink",
    )(dual, change)


def shards(sky_image, measured_real, measured_imaginary, sampling_mask, dual_field):
    channels, row_count, column_count = sky_image.shape
    facets = lax.axis_size("fac")
    width = column_count // facets
    sent = dual_field.reshape(facets, channels, row_count, width)
    coefs = lax.all_to_all(sent, "fac", split_axis=0, concat_axis=0, tiled=True)
    base, synth = fidelity(
        sky_image, measured_real, measured_imaginary, sampling_mask, synthesis_table(width)
    )
    next_image, change = prior(coefs, base, sky_image, synth)
    change = lax.all_to_all(change, "fac", split_axis=0, concat_axis=0, tiled=True)
    next_dual = shrink(dual_field, change.reshape(dual_field.shape))
    return (next_image, next_dual)


def solution(mesh):
    split_channels = P(("groups", "fac"), None, None)
    split_facets = P("groups", None, "fac")
    return jax.shard_map(
        shards,
        mesh=mesh,
        in_specs=(split_channels,) * 4 + (split_facets,),
        out_specs=(split_channels, split_facets),
        check_vma=False,
    )
```

```python
import functools

import jax
import jax.numpy as jnp
import numpy as np
from jax import lax
from jax.experimental import pallas as pl
from jax.experimental.pallas import tpu as pltpu
from jax.sharding import PartitionSpec as P

LEVELS = 4
LANES = 128

low_pass = (
    0.2303778133088964,
    0.7148465705529155,
    0.6308807679298587,
    -0.0279837694168599,
    -0.1870348117190931,
    0.0308413818355607,
    0.0328830116668852,
    -0.010597401785069,
)
high_pass = tuple(((-1) ** tap_index * low_pass[7 - tap_index] for tap_index in range(8)))
primal_step = 0.6
dual_step = 0.8
ball_radius = 12.0
f32 = jnp.float32
bf16 = jnp.bfloat16


def halves(matrix):
    high = np.asarray(matrix, np.float32).astype(bf16)
    low = (np.asarray(matrix, np.float64) - high.astype(np.float64)).astype(bf16)
    return high, low


def split(values):
    high = values.astype(bf16)
    low = (values - high.astype(f32)).astype(bf16)
    return high, low


def mul(left, right):
    return jnp.dot(left, right, preferred_element_type=f32)


def row_fourier(rows):
    grid = np.arange(rows)
    angles = 2.0 * np.pi * (np.outer(grid, grid) % rows) / rows
    return np.concatenate([np.cos(angles), -np.sin(angles)], 0) / np.sqrt(rows)


def lane_fourier(scale):
    grid = np.arange(LANES)
    angles = 2.0 * np.pi * (np.outer(grid, grid) % LANES) / LANES
    cosine, sine = np.cos(angles), np.sin(angles)
    return np.block([[cosine, -sine], [sine, cosine]]) * scale


def twiddles(slabs, columns):
    angles = 2.0 * np.pi * np.outer(np.arange(slabs), np.arange(LANES)) / columns
    table = np.stack([np.cos(angles), -np.sin(angles)], 1)
    return np.broadcast_to(table[:, :, None, :], (slabs, 2, 8, LANES)).astype(np.float32)


def row_wavelet(length):
    current = np.eye(length)
    details = []
    for level_index in range(LEVELS):
        width_now = current.shape[0]
        half_size = width_now // 2
        lower = np.zeros((half_size, width_now))
        upper = np.zeros((half_size, width_now))
        for target in range(half_size):
            for tap_index in range(8):
                lower[target, (2 * target + tap_index) % width_now] += low_pass[tap_index]
                upper[target, (2 * target + tap_index) % width_now] += high_pass[tap_index]
        details.insert(0, upper @ current)
        current = lower @ current
    return np.concatenate([current] + details, 0)


def facet_wavelet(width):
    needed = [width >> LEVELS]
    for level_index in range(LEVELS):
        needed.insert(0, 2 * (needed[0] - 1) + 8)
    current = np.eye(2 * width)
    details = []
    for level_index in range(LEVELS):
        count = needed[level_index + 1]
        lower = np.zeros((count, 2 * width))
        upper = np.zeros((count, 2 * width))
        for target in range(count):
            for tap_index in range(8):
                lower[target] += low_pass[tap_index] * current[2 * target + tap_index]
                upper[target] += high_pass[tap_index] * current[2 * target + tap_index]
        details.insert(0, upper[: width >> (level_index + 1)])
        current = lower
    matrix = np.concatenate([current[: width >> LEVELS]] + details, 0).T
    return np.concatenate([matrix[:width], matrix[width:]], 1)


def turn(value, step, length, sign):
    real, imag = value
    step = step % length
    if step == 0:
        return real, imag
    if 4 * step == length:
        return (-imag, real) if sign > 0 else (imag, -real)
    if 8 * step == length:
        root = float(np.sqrt(0.5))
        if sign > 0:
            return (real - imag) * root, (real + imag) * root
        return (real + imag) * root, (imag - real) * root
    if 8 * step == 3 * length:
        root = float(np.sqrt(0.5))
        if sign > 0:
            return (real + imag) * (-root), (real - imag) * root
        return (imag - real) * root, (real + imag) * (-root)
    cosine = float(np.cos(2.0 * np.pi * step / length))
    sine = float(sign * np.sin(2.0 * np.pi * step / length))
    return real * cosine - imag * sine, real * sine + imag * cosine


def short_transform(values, sign):
    length = len(values)
    if length == 1:
        return values
    even = short_transform(values[0::2], sign)
    odd = short_transform(values[1::2], sign)
    first, second = [], []
    for step in range(length // 2):
        real, imag = turn(odd[step], step, length, sign)
        first.append((even[step][0] + real, even[step][1] + imag))
        second.append((even[step][0] - real, even[step][1] - imag))
    return first + second


def fidelity_kernel(
    sky, real, imag, mask, row_hi, row_lo, back_hi, back_lo, lane_hi, lane_lo,
    inv_hi, inv_lo, twist, early_far, base, early, row_part, slab_part, sem,
):
    rows, columns = sky.shape[1], sky.shape[2]
    slabs = columns // LANES
    width = 512

    @pl.when(pl.program_id(0) == 0)
    def fetch():
        copy = pltpu.make_async_copy(early_far, early, sem)
        copy.start()
        copy.wait()


    def rows_forward(index, carry):
        lanes = pl.ds(pl.multiple_of(index * width, width), width)
        high, low = split(sky[0, :, lanes])
        row_part[:, lanes] = mul(row_hi[...], high) + mul(row_hi[...], low) + mul(row_lo[...], high)
        return carry

    lax.fori_loop(0, columns // width, rows_forward, 0)

    def slabs_forward(index, carry):
        start = pl.multiple_of(index * 8, 8)
        values = []
        for slab in range(slabs):
            lanes = slice(slab * LANES, (slab + 1) * LANES)
            values.append(
                (row_part[pl.ds(start, 8), lanes], row_part[pl.ds(start + rows, 8), lanes])
            )
        for slab, (re, im) in enumerate(short_transform(values, -1)):
            if slab:
                tr, ti = twist[slab, 0], twist[slab, 1]
                re, im = re * tr - im * ti, re * ti + im * tr
            slab_part[slab, pl.ds(start, 8), :LANES] = re
            slab_part[slab, pl.ds(start, 8), LANES:] = im
        return carry

    lax.fori_loop(0, rows // 8, slabs_forward, 0)

    group = 4

    def lanes_both(index, carry):
        pick = pl.ds(index * group, group)
        high, low = split(slab_part[pick].reshape(group * rows, 2 * LANES))
        found = mul(high, lane_hi[...]) + mul(low, lane_hi[...]) + mul(high, lane_lo[...])
        weight = mask[0, pick].reshape(group * rows, LANES).astype(f32)
        re = weight * (found[:, :LANES] - real[0, pick].reshape(group * rows, LANES))
        im = weight * (found[:, LANES:] - imag[0, pick].reshape(group * rows, LANES))
        high, low = split(jnp.concatenate([re, im], 1))
        back = mul(high, inv_hi[...]) + mul(low, inv_hi[...]) + mul(high, inv_lo[...])
        slab_part[pick] = back.reshape(group, rows, 2 * LANES)
        return carry

    lax.fori_loop(0, slabs // group, lanes_both, 0, unroll=True)

    def slabs_back(index, carry):
        start = pl.multiple_of(index * 8, 8)
        values = []
        for slab in range(slabs):
            re = slab_part[slab, pl.ds(start, 8), :LANES]
            im = slab_part[slab, pl.ds(start, 8), LANES:]
            if slab:
                tr, ti = twist[slab, 0], twist[slab, 1]
                re, im = re * tr + im * ti, im * tr - re * ti
            values.append((re, im))
        for slab, (re, im) in enumerate(short_transform(values, 1)):
            lanes = slice(slab * LANES, (slab + 1) * LANES)
            row_part[pl.ds(start, 8), lanes] = re
            row_part[pl.ds(start + rows, 8), lanes] = im
        return carry

    lax.fori_loop(0, rows // 8, slabs_back, 0)

    def rows_back(index, carry):
        lanes = pl.ds(pl.multiple_of(index * width, width), width)
        high, low = split(row_part[:, lanes])
        gradient = mul(back_hi[...], high) + mul(back_hi[...], low) + mul(back_lo[...], high)
        base[0, :, lanes] = sky[0, :, lanes] - primal_step * gradient
        return carry

    lax.fori_loop(0, columns // width, rows_back, 0)


resident = pl.BlockSpec(memory_space=pltpu.VMEM)
distant = pl.BlockSpec(memory_space=pltpu.HBM)


def remote(array):
    return pltpu.with_memory_space_constraint(array, pltpu.HBM)


def whole(array):
    return pl.BlockSpec(array.shape, lambda *index: (0,) * array.ndim)


def fidelity(sky, real, imag, mask, early):
    channels, rows, columns = sky.shape
    slabs = columns // LANES

    def by_slab(values):
        return values.reshape(channels, rows, LANES, slabs).transpose(0, 3, 1, 2)

    forward = row_fourier(rows)
    lane = lane_fourier(1.0 / np.sqrt(columns))
    tables = (
        *halves(forward), *halves(forward.T), *halves(lane), *halves(lane.T),
        twiddles(slabs, columns),
    )
    tables = tuple(remote(jnp.asarray(table)) for table in tables)
    image = pl.BlockSpec((1, rows, columns), lambda c: (c, 0, 0))
    slab = pl.BlockSpec((1, slabs, rows, LANES), lambda c: (c, 0, 0, 0))
    return pl.pallas_call(
        fidelity_kernel,
        out_shape=(
            jax.ShapeDtypeStruct(sky.shape, f32),
            jax.ShapeDtypeStruct(early.shape, early.dtype),
        ),
        grid=(channels,),
        in_specs=[image, slab, slab, slab, *(whole(table) for table in tables), distant],
        out_specs=(image, resident),
        scratch_shapes=[
            pltpu.VMEM((2 * rows, columns), f32),
            pltpu.VMEM((slabs, rows, 2 * LANES), f32),
            pltpu.SemaphoreType.DMA,
        ],
        compiler_params=pltpu.CompilerParams(vmem_limit_bytes=32 << 20),
        name="fidelity",
    )(remote(sky), *(remote(by_slab(values)) for values in (real, imag, mask)), *tables, remote(early))


def prior_kernel(*refs):
    coef, base_far, sky_far, kept = refs[:4]
    tables_far, tables = refs[4:10], refs[12:18]
    image, out = refs[10:12]
    part, turned, held, base, sky, sems, table_sems, synth = refs[18:]
    rowt2, rowt_lo, row2, row_lo, ana2, ana_lo = tables
    facets, channels, rows, width = coef.shape
    synth2, synth_lo = synth.at[: 2 * width], synth.at[2 * width :]
    columns = facets * width
    wide = 4 * width
    batch = 4

    first_table = pltpu.make_async_copy(kept, synth, table_sems.at[len(tables)])
    first_table.start()
    fetches = [
        pltpu.make_async_copy(tables_far[index], tables[index], table_sems.at[index])
        for index in range(len(tables))
    ]
    loads = [
        (
            pltpu.make_async_copy(base_far.at[channel], base.at[channel], sems.at[0, channel]),
            pltpu.make_async_copy(sky_far.at[channel], sky.at[channel], sems.at[1, channel]),
        )
        for channel in range(channels)
    ]
    for copy in (*fetches[:2], *loads[0], *fetches[2:], *loads[1]):
        copy.start()
    copies = []

    first_table.wait()
    for channel in range(channels):

        before = None
        for first in range(0, facets, batch):
            high, low = split(coef[first : first + batch, channel].reshape(batch * rows, width))
            both = mul(jnp.concatenate([high, low], 1), synth2[...]) + mul(high, synth_lo[...])
            for index in range(batch):
                facet = first + index
                mine = both[index * rows : (index + 1) * rows]
                if facet:
                    high, low = split(mine[:, :width] + before)
                    lanes = slice(facet * width, (facet + 1) * width)
                    part[channel, :rows, lanes] = high
                    part[channel, rows:, lanes] = low
                else:
                    held[...] = mine[:, :width]
                before = mine[:, width:]
        high, low = split(held[...] + before)
        part[channel, :rows, :width] = high
        part[channel, rows:, :width] = low

    for copy in fetches[:2]:
        copy.wait()
    for channel in range(channels):
        for copy in loads[channel]:
            copy.wait()
        for start in range(0, columns, wide):
            lanes = slice(start, start + wide)
            both = part[channel, :, lanes]
            step = mul(rowt2[...], both) + mul(rowt_lo[...], both[:rows])
            fresh = jnp.maximum(base[channel, :, lanes] - step, 0.0)
            base[channel, :, lanes] = fresh
            high, low = split(2.0 * fresh - sky[channel, :, lanes])
            part[channel, :rows, lanes] = high
            part[channel, rows:, lanes] = low
        copy = pltpu.make_async_copy(base.at[channel], image.at[channel], sems.at[2, channel])
        copy.start()
        copies.append(copy)

        if channel == 0:
            for copy in fetches[2:]:
                copy.wait()
        for start in range(0, columns, wide):
            lanes = slice(start, start + wide)
            both = part[channel, :, lanes]
            high, low = split(mul(row2[...], both) + mul(row_lo[...], both[:rows]))
            for index in range(wide // width):
                mine = slice(index * width, (index + 1) * width)
                turned[channel, start // width + index, :, :width] = high[:, mine]
                turned[channel, start // width + index, :, width:] = low[:, mine]

        before = None
        for first in range(0, facets, batch):
            values = turned[channel, first : first + batch].reshape(batch * rows, 2 * width)
            both = mul(values, ana2[...]) + mul(values[:, :width], ana_lo[...])
            for index in range(batch):
                facet = first + index
                mine = both[index * rows : (index + 1) * rows]
                if facet:
                    out[facet - 1, channel] = before + mine[:, width:]
                else:
                    held[...] = mine[:, width:]
                before = mine[:, :width]
        out[facets - 1, channel] = before + held[...]

    for copy in copies:
        copy.wait()


def synthesis_table(width):
    facet_table = facet_wavelet(width)
    own, other = facet_table[:, :width], facet_table[:, width:]
    high, low = halves(np.concatenate([own.T, other.T], 1))
    return jnp.asarray(np.concatenate([high, high, low], 0))


def prior(coefs, base, sky, synth):
    channels, rows, columns = sky.shape
    facets, width = coefs.shape[0], coefs.shape[3]
    facet_table = facet_wavelet(width)
    analysis = halves(dual_step * facet_table)
    row_table = row_wavelet(rows)
    rowt = halves(primal_step * row_table.T)
    row = halves(row_table)
    tables = (
        np.concatenate([rowt[0], rowt[0]], 1), rowt[1],
        np.concatenate([row[0], row[0]], 1), row[1],
        np.concatenate([analysis[0], analysis[0]], 0), analysis[1],
    )
    tables = tuple(remote(jnp.asarray(table)) for table in tables)
    return pl.pallas_call(
        prior_kernel,
        out_shape=(
            jax.ShapeDtypeStruct(sky.shape, f32),
            jax.ShapeDtypeStruct(coefs.shape, f32),
        ),
        in_specs=[resident, distant, distant, resident, *(distant for table in tables)],
        out_specs=(distant, resident),
        scratch_shapes=[
            *(pltpu.VMEM(table.shape, bf16) for table in tables),
            pltpu.VMEM((channels, 2 * rows, columns), bf16),
            pltpu.VMEM((channels, facets, rows, 2 * width), bf16),
            pltpu.VMEM((rows, width), f32),
            pltpu.VMEM(sky.shape, f32),
            pltpu.VMEM(sky.shape, f32),
            pltpu.SemaphoreType.DMA((3, channels)),
            pltpu.SemaphoreType.DMA((len(tables) + 1,)),
            pltpu.VMEM(synth.shape, bf16),
        ],
        compiler_params=pltpu.CompilerParams(vmem_limit_bytes=20 << 20),
        name="prior",
    )(coefs, remote(base), remote(sky), synth, *tables)


def shrink_kernel(dual, change, out_far, out, sems):
    channels = dual.shape[0]
    some = channels // sems.shape[0]
    total = 0.0
    for channel in range(channels):
        lifted = dual[channel] + change[channel]
        total = total + lifted * lifted
    scale = 1.0 / jnp.maximum(1.0, jnp.sqrt(total) / ball_radius)
    copies = []
    for first in range(0, channels, some):
        for channel in range(first, first + some):
            out[channel] = (dual[channel] + change[channel]) * scale
        pick = pl.ds(first, some)
        copy = pltpu.make_async_copy(out.at[pick], out_far.at[pick], sems.at[first // some])
        copy.start()
        copies.append(copy)
    for copy in copies:
        copy.wait()


def shrink(dual, change):
    return pl.pallas_call(
        shrink_kernel,
        out_shape=jax.ShapeDtypeStruct(dual.shape, f32),
        in_specs=[resident, resident],
        out_specs=distant,
        scratch_shapes=[pltpu.VMEM(dual.shape, f32), pltpu.SemaphoreType.DMA((16,))],
        compiler_params=pltpu.CompilerParams(vmem_limit_bytes=6 << 20),
        name="shrink",
    )(dual, change)


def shards(sky_image, measured_real, measured_imaginary, sampling_mask, dual_field):
    channels, row_count, column_count = sky_image.shape
    facets = lax.axis_size("fac")
    width = column_count // facets
    sent = dual_field.reshape(facets, channels, row_count, width)
    coefs = lax.all_to_all(sent, "fac", split_axis=0, concat_axis=0, tiled=True)
    base, synth = fidelity(
        sky_image, measured_real, measured_imaginary, sampling_mask, synthesis_table(width)
    )
    next_image, change = prior(coefs, base, sky_image, synth)
    change = lax.all_to_all(change, "fac", split_axis=0, concat_axis=0, tiled=True)
    next_dual = shrink(dual_field, change.reshape(dual_field.shape))
    return (next_image, next_dual)


def solution(mesh):
    split_channels = P(("groups", "fac"), None, None)
    split_facets = P("groups", None, "fac")
    return jax.shard_map(
        shards,
        mesh=mesh,
        in_specs=(split_channels,) * 4 + (split_facets,),
        out_specs=(split_channels, split_facets),
        check_vma=False,
    )
```
